32 devices in a mesh: grp: 2 (over y), lab: 4 (over z), dp: 2 (over x), sub: 2 (over core).
Axes of the slice: x: 2, y: 2, z: 4, core: 2. Of those that a mesh axis runs over, the one named last changes fastest.
Arguments:
- enc_rows: bfloat16 [4096, 2048], P(('grp', 'lab', 'dp'), 'sub'), parts along dimension 0, may hold values from -6 to 6
- shortlist: int32 [4096, 8], P(('grp', 'lab', 'dp')), parts along dimension 0, may hold values from 0 to 15, all different within a row; in each aligned block of 256 rows (0 to 255, 256 to 511, ...) at most 256 rows name the same one
- cluster_slot: int32 [16], replicated, may hold values from 0 to 15, each once
- positives: int32 [4096, 16], P(('grp', 'lab', 'dp')), parts along dimension 0, may hold values from 0 to 2047
- panels: bfloat16 [16, 2048, 256], P('lab', 'sub'), may hold values from -0.125 to 0.125
Outputs:
- enc_grad: bfloat16 [4096, 2048], P(('grp', 'lab', 'dp'), 'sub'), parts along dimension 0
- panel_grad: float32 [32, 2048, 256], P(('grp', 'lab', 'dp'), 'sub'), parts along dimension 0
The draws below stay inside these ranges and needn't reach their ends.
There are 2 independent parts, one for each index of `grp`. The reference program is written for one: setup_inputs(seed, part) draws one part's arguments, and reference() takes and returns one part's arrays. A program takes and returns all parts, laid end to end along the dimension named above; an argument that names none is the same for every part. Nothing has to cross between parts.
Inputs may be any that keep to these rules, and one draw needn't show every extreme that they name: `shortlist`: each sample names 8 different clusters. Among the 256 samples of one device (aligned blocks of rows, in order), no cluster is named more than 256 times; in some such blocks a cluster is named exactly 256 times. `cluster_slot`: each panel index occurs once. `positives`: A value v stands for label v % 256 of the sample's shortlisted cluster number v // 256; values may repeat.
All inputs are finite; a program needn't handle non-finite values.
Results may differ from the reference program's by a relative error of at most 0.011.
Values may be sent and summed in bfloat16 or wider, within the bound.
A program may use at most 128 MiB of HBM per device.

```python
import math
import jax
import jax.numpy as jnp
import numpy as np
from jax import lax

H = 2048
B = 256
K = 8
P_SIZE = 16
S_DEV = 256
SAMPLES = 2048
CLUSTERS = 16
MOST = 256


def place_ends(drawn, own_key, low, high):
    extent = drawn.shape
    spot = [jax.random.randint(jax.random.fold_in(own_key, axis), (), 0, extent[axis]) for axis in range(len(extent))]
    drawn = drawn.at[tuple(spot)].set(low)
    longest = extent.index(max(extent))
    spot[longest] = (spot[longest] + 1) % extent[longest]
    return drawn.at[tuple(spot)].set(high)


def block_levels(key, extent, split, least, top_value):
    def one(dim, blocks):
        draws = jax.random.uniform(jax.random.fold_in(jax.random.fold_in(key, 6), dim), (blocks,), jnp.float32, least / len(split), top_value / len(split))
        return jnp.repeat(jnp.exp(draws), extent[dim] // blocks).reshape((-1,) + (1,) * (len(extent) - dim - 1))

    loudness = one(*split[0])
    for cut in split[1:]:
        loudness = loudness * one(*cut)
    return loudness


def assign_block(rng, own, number, rows, number_of, top, limit, skew):
    sequence = jax.random.permutation(rng, number_of)
    crowded, common = portions_of(number_of, rows * top, limit, skew, True), portions_of(number_of, rows * top, limit, skew, False)
    places = jnp.arange(number_of)

    def named(lengths, rotation):
        used = int((lengths > 0).sum())
        fixed = max(1, used // 4)
        moved = fixed + (places - fixed + rotation * (used - fixed)) % max(1, number_of - fixed)
        return jnp.zeros((number_of,), jnp.int32).at[sequence[jnp.where(places < fixed, places, moved)]].set(jnp.asarray(lengths, jnp.int32))

    lengths = jnp.where(number % 4 == 0, named(crowded, number // 4), named(common, number - number // 4 - 1))
    mixed = jax.random.permutation(jax.random.fold_in(own, 3), number_of)
    donor, sink = mixed[0:number_of // 2 * 2:2], mixed[1:number_of // 2 * 2:2]
    slack = jnp.minimum(lengths[donor] - 1, limit - lengths[sink]) // 2
    slack = jnp.where((donor == sequence[0]) | (sink == sequence[0]) | (lengths[sink] == 0), 0, jnp.maximum(slack, 0))
    moved = jax.random.randint(jax.random.fold_in(own, 4), (number_of // 2,), 0, 1 << 20) % (slack + 1)
    lengths = lengths.at[donor].add(-moved).at[sink].add(moved)
    items = jnp.searchsorted(jnp.cumsum(lengths), jnp.arange(rows * top), side="right").astype(jnp.int32)
    table = items.reshape(top, rows).T
    table = table[jax.random.permutation(jax.random.fold_in(own, 1), rows)]
    rotation = jax.random.randint(jax.random.fold_in(own, 2), (rows, 1), 0, top)
    return jnp.take_along_axis(table, (jnp.arange(top)[None, :] + rotation) % top, axis=1)


def portions_of(count, total, most, skew, full):
    portions = [(1 << 20) // math.isqrt(rank ** skew) + 1 for rank in range(1, count + 1)]
    largest = most if full else min(most, max(-(-total // count), total * portions[0] // sum(portions)))
    least = 1 if total - largest >= count - 1 else 0
    holding, rest = [largest] + [least] * (count - 1), total - largest - least * (count - 1)
    while rest > 0:
        free = [i for i in range(1, count) if holding[i] < largest] or [i for i in range(1, count) if holding[i] < most]
        pool, remaining = sum([portions[i] for i in free]), rest
        for i in free:
            extra = min(most - holding[i], max(1, remaining * portions[i] // pool), rest)
            holding[i] = holding[i] + extra
            rest = rest - extra
    return np.array(holding)


def normal_values(rng, shape, scale, limit, split=(), held_as=jnp.bfloat16):
    factor_of = block_levels(rng, shape, split, -0.22, 0.18) if split else 1.0
    result = jax.random.normal(rng, shape, jnp.float32) * scale * factor_of
    return jnp.minimum(jnp.maximum(result, -limit), limit).astype(held_as)


def setup_inputs(seed: int = 0, part: int = 0) -> dict:
    splits = jax.random.split(jax.random.key(seed), 6)
    part_keys = jax.random.split(jax.random.fold_in(splits[5], part), 6)
    enc_rows = normal_values(part_keys[0], (SAMPLES, H), 1.0, 6.0, ((0, 8), (1, 2)))
    shortlist_keys = jax.random.split(jax.random.fold_in(part_keys[1], 1), SAMPLES // S_DEV)
    shortlist_turns = jax.random.permutation(jax.random.fold_in(part_keys[1], 3), SAMPLES // S_DEV)
    shortlist = jax.vmap(lambda own, number: assign_block(jax.random.fold_in(part_keys[1], 2), own, number, S_DEV, CLUSTERS, K, MOST, 2))(shortlist_keys, shortlist_turns).reshape((SAMPLES, K))
    cluster_slot = jax.random.permutation(splits[2], CLUSTERS).astype(jnp.int32)
    positives = place_ends(jax.random.randint(part_keys[3], (SAMPLES, P_SIZE), 0, K * B), jax.random.fold_in(part_keys[3], 1), 0, (K * B) - 1).astype(jnp.int32)
    panels = normal_values(splits[4], (CLUSTERS, H, B), H ** -0.5, 0.125, ((0, 4), (1, 2)))
    return dict(enc_rows=enc_rows, shortlist=shortlist, cluster_slot=cluster_slot, positives=positives, panels=panels)


def reference(enc_rows, shortlist, cluster_slot, positives, panels):
    shards = SAMPLES // S_DEV
    pair_total = SAMPLES * K
    slot = jnp.take(cluster_slot, shortlist, axis=0).astype(jnp.int32)
    flat_slot = slot.reshape(shards, S_DEV * K)
    cluster_ids = jnp.arange(CLUSTERS, dtype=jnp.int32)
    placed = (flat_slot[:, :, None] == cluster_ids[None, None, :]).astype(jnp.int32)
    ranking = jnp.sum((jnp.cumsum(placed, axis=1) - 1) * placed, axis=2)
    place = jnp.arange(shards, dtype=jnp.int32)[:, None] * MOST + ranking
    table = jnp.full((CLUSTERS, shards * MOST), -1, jnp.int32)
    table = table.at[flat_slot.reshape(-1), place.reshape(-1)].set(jnp.arange(pair_total, dtype=jnp.int32))
    label_ids = jnp.arange(B, dtype=jnp.int32)

    def per_cluster(total, inputs):
        entries, weight = inputs
        present = entries >= 0
        source = jnp.maximum(entries, 0)
        sample = (source // K).astype(jnp.int32)
        beam_pos = (source % K).astype(jnp.int32)
        picked = jnp.take(enc_rows, sample, axis=0)
        picked = jnp.where(present[:, None], picked, jnp.zeros((), enc_rows.dtype))
        logits = jnp.dot(picked, weight, preferred_element_type=jnp.float32)
        wanted = jnp.take(positives, sample, axis=0) - (beam_pos * B)[:, None]
        target = jnp.any(wanted[:, :, None] == label_ids[None, None, :], axis=1)
        target = jnp.logical_and(target, present[:, None]).astype(jnp.float32)
        logit_grad = (jax.nn.sigmoid(logits) - target).astype(jnp.bfloat16)
        pair_grad = jnp.dot(logit_grad, weight.T, preferred_element_type=jnp.float32).astype(jnp.bfloat16)
        addend = jnp.where(present[:, None], pair_grad.astype(jnp.float32), jnp.zeros((), jnp.float32))
        total = total.at[sample].add(addend)
        panel_part = jnp.dot(picked.T, logit_grad, preferred_element_type=jnp.float32)
        return total, panel_part

    start = jnp.zeros((SAMPLES, H), jnp.float32)
    total, panel_grad = lax.scan(per_cluster, start, (table, panels))
    return total.astype(jnp.bfloat16), panel_grad
```

```python
import jax
import jax.numpy as jnp
from jax import lax
from jax.sharding import PartitionSpec as P


def label_slots(shortlist, cluster_slot, positives, label_width):
    clusters = jnp.arange(cluster_slot.shape[0], dtype=jnp.int32)
    named = (shortlist[:, :, None] == clusters).astype(jnp.int32)
    slots = jnp.sum(named * cluster_slot, axis=2)
    beams = jnp.arange(shortlist.shape[1], dtype=jnp.int32)
    picked = (positives[:, :, None] // label_width == beams).astype(jnp.int32)
    pos_slot = jnp.sum(picked * slots[:, None, :], axis=2)
    return slots, pos_slot, positives % label_width


def body(enc_rows, shortlist, cluster_slot, positives, panels):
    samples, half = enc_rows.shape
    own, _, width = panels.shape
    labs = lax.axis_size("lab")
    slots, pos_slot, pos_col = label_slots(shortlist, cluster_slot, positives, width)
    ids = jnp.concatenate([slots, pos_slot * width + pos_col], axis=1)
    all_ids = lax.all_gather(ids, "lab", axis=0, tiled=True)
    all_rows = lax.all_gather(enc_rows, "lab", axis=0, tiled=True)
    beam = shortlist.shape[1]
    first = lax.axis_index("lab") * own
    columns = first * width + jnp.arange(own * width, dtype=jnp.int32)
    present = jnp.any(all_ids[:, :beam, None] == columns[None, None, :] // width, axis=1)
    target = jnp.any(all_ids[:, beam:, None] == columns[None, None, :], axis=1)
    flat = panels.transpose(1, 0, 2).reshape(half, own * width)
    partial = jnp.dot(all_rows, flat, preferred_element_type=jnp.float32)
    logits = lax.psum(partial, "sub")
    grad = jnp.where(present, jax.nn.sigmoid(logits) - target.astype(jnp.float32), 0.0)
    grad = grad.astype(jnp.bfloat16)
    back = lax.dot_general(
        grad, flat, (((1,), (1,)), ((), ())), preferred_element_type=jnp.float32
    ).astype(jnp.bfloat16)
    returned = lax.all_to_all(
        back.reshape(labs, samples, half), "lab", split_axis=0, concat_axis=0, tiled=True
    )
    enc_grad = jnp.sum(returned, axis=0, dtype=jnp.float32).astype(jnp.bfloat16)
    part = jnp.einsum(
        "rh,rcb->chb",
        all_rows,
        grad.reshape(labs * samples, own, width),
        preferred_element_type=jnp.float32,
    )
    panel_grad = lax.psum_scatter(part, "dp", scatter_dimension=0, tiled=True)
    return enc_grad, panel_grad


def solution(mesh):
    in_specs = (
        P(("grp", "lab", "dp"), "sub"),
        P(("grp", "lab", "dp"), None),
        P(),
        P(("grp", "lab", "dp"), None),
        P("lab", "sub", None),
    )
    out_specs = (P(("grp", "lab", "dp"), "sub"), P(("grp", "lab", "dp"), "sub", None))
    return jax.shard_map(body, mesh=mesh, in_specs=in_specs, out_specs=out_specs, check_vma=False)
```

```python
import functools

import jax
import jax.numpy as jnp
from jax import lax
from jax.experimental import pallas as pl
from jax.experimental.pallas import tpu as pltpu
from jax.sharding import PartitionSpec as P


def label_slots(shortlist, cluster_slot, positives, label_width):
    clusters = jnp.arange(cluster_slot.shape[0], dtype=jnp.int32)
    named = (shortlist[:, :, None] == clusters).astype(jnp.int32)
    slots = jnp.sum(named * cluster_slot, axis=2)
    beams = jnp.arange(shortlist.shape[1], dtype=jnp.int32)
    picked = (positives[:, :, None] // label_width == beams).astype(jnp.int32)
    pos_slot = jnp.sum(picked * slots[:, None, :], axis=2)
    return slots, pos_slot, positives % label_width


def array_body(enc_rows, shortlist, cluster_slot, positives, panels):
    samples, half = enc_rows.shape
    own, _, width = panels.shape
    labs = lax.axis_size("lab")
    slots, pos_slot, pos_col = label_slots(shortlist, cluster_slot, positives, width)
    ids = jnp.concatenate([slots, pos_slot * width + pos_col], axis=1)
    all_ids = lax.all_gather(ids, "lab", axis=0, tiled=True)
    all_rows = lax.all_gather(enc_rows, "lab", axis=0, tiled=True)
    beam = shortlist.shape[1]
    first = lax.axis_index("lab") * own
    columns = first * width + jnp.arange(own * width, dtype=jnp.int32)
    present = jnp.any(all_ids[:, :beam, None] == columns[None, None, :] // width, axis=1)
    target = jnp.any(all_ids[:, beam:, None] == columns[None, None, :], axis=1)
    flat = panels.transpose(1, 0, 2).reshape(half, own * width)
    partial = jnp.dot(all_rows, flat, preferred_element_type=jnp.float32)
    logits = lax.psum(partial, "sub")
    grad = jnp.where(present, jax.nn.sigmoid(logits) - target.astype(jnp.float32), 0.0)
    grad = grad.astype(jnp.bfloat16)
    back = lax.dot_general(
        grad, flat, (((1,), (1,)), ((), ())), preferred_element_type=jnp.float32
    ).astype(jnp.bfloat16)
    returned = lax.all_to_all(
        back.reshape(labs, samples, half), "lab", split_axis=0, concat_axis=0, tiled=True
    )
    enc_grad = jnp.sum(returned, axis=0, dtype=jnp.float32).astype(jnp.bfloat16)
    part = jnp.einsum(
        "rh,rcb->chb",
        all_rows,
        grad.reshape(labs * samples, own, width),
        preferred_element_type=jnp.float32,
    )
    panel_grad = lax.psum_scatter(part, "dp", scatter_dimension=0, tiled=True)
    return enc_grad, panel_grad


CUTS = 2
MESH = pl.DeviceIdType.MESH


def unit_of(u, me, labs):
    pairs = jnp.minimum(me, labs - 1 - me)
    longer = jnp.where(2 * me < labs - 1, 1, -1)
    v = u - CUTS
    w = v % (2 * CUTS)
    near = me + (v // (2 * CUTS) + 1) * (2 * (w % 2) - 1)
    x = v - 2 * CUTS * pairs
    far = me + longer * (pairs + 1 + x // CUTS)
    block = jnp.where(u < CUTS, me, jnp.where(x < 0, near, far))
    cut = jnp.where(u < CUTS, u, jnp.where(x < 0, w // 2, x % CUTS))
    return block, cut


def step_kernel(
    dims, enc_ref, ids_ref, panel_ref, enc_out, panel_out,
    rows, rows_t, ids_buf, part, other, want, grads, held, sent, got, share_out, share_in,
    row_send, row_recv, id_send, id_recv, lx_send, lx_recv, rt_send, rt_recv, sh_send, sh_recv,
):
    labs, dps, own, beam, picks, width = dims
    size = enc_ref.shape[1]
    half = enc_ref.shape[2]
    me = lax.axis_index("lab")
    dp = lax.axis_index("dp")
    core = lax.axis_index("sub")
    left, right = jnp.maximum(me - 1, 0), jnp.minimum(me + 1, labs - 1)
    keep = own // dps

    barrier = pltpu.get_barrier_semaphore()
    for off in range(1, labs):
        pl.semaphore_signal(barrier, inc=1, device_id={"lab": (me + off) % labs}, device_id_type=MESH)
    for off in range(1, dps):
        pl.semaphore_signal(barrier, inc=1, device_id={"dp": (dp + off) % dps}, device_id_type=MESH)
    pl.semaphore_signal(barrier, inc=1, device_id={"sub": 1 - core}, device_id_type=MESH)
    pl.semaphore_wait(barrier, labs + dps - 1)

    def remote(src, dst, send, recv, where):
        return pltpu.make_async_remote_copy(
            src_ref=src, dst_ref=dst, send_sem=send, recv_sem=recv,
            device_id=where, device_id_type=MESH,
        )

    def row_copy(src, block, cut, side):
        return remote(
            src, rows.at[block, cut], row_send.at[side, block, cut], row_recv.at[block, cut],
            {"lab": left if side == 0 else right},
        )

    def id_copy(off):
        return remote(
            ids_ref, ids_buf.at[me], id_send.at[off], id_recv.at[me], {"lab": (me + off) % labs}
        )

    def id_arrival(block):
        return remote(ids_ref, ids_buf.at[block], id_send.at[0], id_recv.at[block], {"lab": left})

    def lx_copy(block, cut):
        return remote(
            part.at[block, cut], other.at[block, cut],
            lx_send.at[block, cut], lx_recv.at[block, cut], {"sub": 1 - core},
        )

    def back_copy(block, cut, side):
        return remote(
            sent.at[block, cut], got.at[side, block, cut],
            rt_send.at[block, cut], rt_recv.at[side, block, cut],
            {"lab": right if side == 0 else left},
        )

    def share_copy(off, j):
        return remote(
            share_out.at[off - 1, j], share_in.at[off - 1, j],
            sh_send.at[off - 1, j], sh_recv.at[off - 1, j], {"dp": (dp + off) % dps},
        )

    for off in range(1, labs):
        id_copy(off).start()
    for cut in range(CUTS):
        @pl.when(me > 0)
        def _():
            row_copy(enc_ref.at[cut], me, cut, 0).start()

        @pl.when(me < labs - 1)
        def _():
            row_copy(enc_ref.at[cut], me, cut, 1).start()

    rows[me] = enc_ref[...]
    ids_buf[me] = ids_ref[...]
    lane = lax.broadcasted_iota(jnp.int32, (1, width), 1).astype(jnp.float32)

    @pl.loop(0, labs * CUTS)
    def _(u):
        block, cut = unit_of(u, me, labs)

        @pl.when(block != me)
        def _():
            row_copy(enc_ref.at[0], block, cut, 0).wait_recv()

        @pl.when((block < me) & (me < labs - 1))
        def _():
            row_copy(rows.at[block, cut], block, cut, 1).start()

        @pl.when((block > me) & (me > 0))
        def _():
            row_copy(rows.at[block, cut], block, cut, 0).start()

        unit = rows[block, cut]
        for c in range(own):
            part[block, cut, :, c * width:(c + 1) * width] = jnp.dot(
                unit, panel_ref[c], preferred_element_type=jnp.float32
            )
        lx_copy(block, cut).start()
        rows_t[block, cut] = unit.T

        @pl.when((block != me) & (cut == 0))
        def _():
            id_arrival(block).wait_recv()

        ids = ids_buf[block, cut]
        ids = jnp.concatenate([ids, jnp.zeros((128 - ids.shape[0], size), jnp.float32)], axis=0).T
        for c in range(own):
            slot = (me * own + c).astype(jnp.float32)
            present = jnp.zeros((size, 1), jnp.bool_)
            for k in range(beam):
                present = present | (ids[:, k:k + 1] == slot)
            here = lane + slot * width
            target = jnp.zeros((size, width), jnp.float32)
            for i in range(beam, beam + picks):
                target = jnp.where(ids[:, i:i + 1] == here, 1.0, target)
            want[:, c * width:(c + 1) * width] = jnp.where(present, target, 2.0)

        lx_copy(block, cut).wait_recv()
        total = jnp.zeros((size, half), jnp.float32)
        for c in range(own):
            cols = slice(c * width, (c + 1) * width)
            logit = part[block, cut, :, cols] + other[block, cut, :, cols]
            goal = want[:, cols]
            grad = jnp.where(goal > 1.5, 0.0, jax.nn.sigmoid(logit) - goal).astype(jnp.bfloat16)
            grads[block, cut, :, cols] = grad
            total += lax.dot_general(
                grad, panel_ref[c], (((1,), (1,)), ((), ())), preferred_element_type=jnp.float32
            )
        held[block, cut] = total

        @pl.when((me == 0) & (block > 0))
        def _():
            sent[block, cut] = total.astype(jnp.bfloat16)
            back_copy(block, cut, 0).start()

        @pl.when((me == labs - 1) & (block < me))
        def _():
            sent[block, cut] = total.astype(jnp.bfloat16)
            back_copy(block, cut, 1).start()

    units = [(b, q) for b in range(labs) for q in range(CUTS)]

    def panel_sum(c):
        wide = jnp.concatenate([rows_t[b, q] for b, q in units], axis=1)
        tall = jnp.concatenate(
            [grads[b, q, :, pl.ds(pl.multiple_of(c * width, width), width)] for b, q in units],
            axis=0,
        )
        return jnp.dot(wide, tall, preferred_element_type=jnp.float32)

    for off in range(1, dps):
        for j in range(keep):
            share_out[off - 1, j] = panel_sum(((dp + off) % dps) * keep + j).astype(jnp.bfloat16)
            share_copy(off, j).start()
    for j in range(keep):
        panel_out[j] = panel_sum(dp * keep + j)

    def pass_on(block, cut, side):
        back_copy(block, cut, side).wait_recv()
        sent[block, cut] = (
            held[block, cut] + got[side, block, cut].astype(jnp.float32)
        ).astype(jnp.bfloat16)
        back_copy(block, cut, side).start()

    for k in range(1, labs):
        for cut in range(CUTS):
            @pl.when((me > 0) & (me < k))
            def _():
                pass_on(k, cut, 0)

            @pl.when((me > labs - 1 - k) & (me < labs - 1))
            def _():
                pass_on(labs - 1 - k, cut, 1)

    for cut in range(CUTS):
        @pl.when(me > 0)
        def _():
            back_copy(me, cut, 0).wait_recv()
            held[me, cut] += got[0, me, cut].astype(jnp.float32)

        @pl.when(me < labs - 1)
        def _():
            back_copy(me, cut, 1).wait_recv()
            held[me, cut] += got[1, me, cut].astype(jnp.float32)

        enc_out[cut] = held[me, cut].astype(jnp.bfloat16)

    for off in range(1, dps):
        for j in range(keep):
            share_copy(off, j).wait_recv()
            panel_out[j] += share_in[off - 1, j].astype(jnp.float32)

    for off in range(1, labs):
        id_copy(off).wait_send()
    for off in range(1, dps):
        for j in range(keep):
            share_copy(off, j).wait_send()
    for block, cut in units:
        lx_copy(block, cut).wait_send()

        @pl.when((block <= me) & (me < labs - 1))
        def _():
            row_copy(enc_ref.at[0], block, cut, 1).wait_send()

        @pl.when((block >= me) & (me > 0))
        def _():
            row_copy(enc_ref.at[0], block, cut, 0).wait_send()

        @pl.when(block != me)
        def _():
            back_copy(block, cut, 0).wait_send()


def kernel_body(enc_rows, shortlist, cluster_slot, positives, panels):
    samples, half = enc_rows.shape
    own, _, width = panels.shape
    labs, dps = lax.axis_size("lab"), lax.axis_size("dp")
    beam, picks = shortlist.shape[1], positives.shape[1]
    size = samples // CUTS
    keep = own // dps
    slots, pos_slot, pos_col = label_slots(shortlist, cluster_slot, positives, width)
    ids = jnp.concatenate([slots, pos_slot * width + pos_col], axis=1).astype(jnp.float32)
    id_rows = -(-(beam + picks) // 8) * 8
    ids = jnp.pad(ids, ((0, 0), (0, id_rows - beam - picks)), constant_values=-1.0)
    ids = ids.reshape(CUTS, size, id_rows).transpose(0, 2, 1)
    f32, bf16 = jnp.float32, jnp.bfloat16
    vmem, dma = pltpu.VMEM, pltpu.SemaphoreType.DMA
    whole = pl.BlockSpec(memory_space=pltpu.VMEM)
    enc_grad, panel_grad = pl.pallas_call(
        functools.partial(step_kernel, (labs, dps, own, beam, picks, width)),
        out_shape=(
            jax.ShapeDtypeStruct((CUTS, size, half), bf16),
            jax.ShapeDtypeStruct((keep, half, width), f32),
        ),
        in_specs=[whole] * 3,
        out_specs=(whole, whole),
        scratch_shapes=[
            vmem((labs, CUTS, size, half), bf16),
            vmem((labs, CUTS, half, size), bf16),
            vmem((labs, CUTS, id_rows, size), f32),
            vmem((labs, CUTS, size, own * width), f32),
            vmem((labs, CUTS, size, own * width), f32),
            vmem((size, own * width), f32),
            vmem((labs, CUTS, size, own * width), bf16),
            vmem((labs, CUTS, size, half), f32),
            vmem((labs, CUTS, size, half), bf16),
            vmem((2, labs, CUTS, size, half), bf16),
            vmem((dps - 1, keep, half, width), bf16),
            vmem((dps - 1, keep, half, width), bf16),
            dma((2, labs, CUTS)),
            dma((labs, CUTS)),
            dma((labs,)),
            dma((labs,)),
            dma((labs, CUTS)),
            dma((labs, CUTS)),
            dma((labs, CUTS)),
            dma((2, labs, CUTS)),
            dma((dps - 1, keep)),
            dma((dps - 1, keep)),
        ],
        compiler_params=pltpu.CompilerParams(
            collective_id=0, has_side_effects=True, vmem_limit_bytes=58 << 20
        ),
    )(enc_rows.reshape(CUTS, size, half), ids, panels)
    return enc_grad.reshape(samples, half), panel_grad


def kernel_fits(enc_rows, shortlist, positives, panels):
    samples, half = enc_rows.shape
    own, _, width = panels.shape
    labs, dps = lax.axis_size("lab"), lax.axis_size("dp")
    unit = labs * samples
    room = unit * half * 14 + unit * own * width * 10 + 14 * own * half * width
    return (
        room < 54 << 20
        and labs > 1
        and dps > 1
        and lax.axis_size("sub") == 2
        and own % dps == 0
        and samples % (CUTS * 128) == 0
        and half % 128 == 0
        and width % 128 == 0
        and shortlist.shape[1] + positives.shape[1] <= 128
    )


def body(enc_rows, shortlist, cluster_slot, positives, panels):
    if kernel_fits(enc_rows, shortlist, positives, panels):
        return kernel_body(enc_rows, shortlist, cluster_slot, positives, panels)
    return array_body(enc_rows, shortlist, cluster_slot, positives, panels)


def solution(mesh):
    in_specs = (
        P(("grp", "lab", "dp"), "sub"),
        P(("grp", "lab", "dp"), None),
        P(),
        P(("grp", "lab", "dp"), None),
        P("lab", "sub", None),
    )
    out_specs = (P(("grp", "lab", "dp"), "sub"), P(("grp", "lab", "dp"), "sub", None))
    return jax.shard_map(body, mesh=mesh, in_specs=in_specs, out_specs=out_specs, check_vma=False)
```

```python
import functools

import jax
import jax.numpy as jnp
from jax import lax
from jax.experimental import pallas as pl
from jax.experimental.pallas import tpu as pltpu
from jax.sharding import PartitionSpec as P


def label_slots(shortlist, cluster_slot, positives, label_width):
    clusters = jnp.arange(cluster_slot.shape[0], dtype=jnp.int32)
    named = (shortlist[:, :, None] == clusters).astype(jnp.int32)
    slots = jnp.sum(named * cluster_slot, axis=2)
    beams = jnp.arange(shortlist.shape[1], dtype=jnp.int32)
    picked = (positives[:, :, None] // label_width == beams).astype(jnp.int32)
    pos_slot = jnp.sum(picked * slots[:, None, :], axis=2)
    return slots, pos_slot, positives % label_width


def array_body(enc_rows, shortlist, cluster_slot, positives, panels):
    samples, half = enc_rows.shape
    own, _, width = panels.shape
    labs = lax.axis_size("lab")
    slots, pos_slot, pos_col = label_slots(shortlist, cluster_slot, positives, width)
    ids = jnp.concatenate([slots, pos_slot * width + pos_col], axis=1)
    all_ids = lax.all_gather(ids, "lab", axis=0, tiled=True)
    all_rows = lax.all_gather(enc_rows, "lab", axis=0, tiled=True)
    beam = shortlist.shape[1]
    first = lax.axis_index("lab") * own
    columns = first * width + jnp.arange(own * width, dtype=jnp.int32)
    present = jnp.any(all_ids[:, :beam, None] == columns[None, None, :] // width, axis=1)
    target = jnp.any(all_ids[:, beam:, None] == columns[None, None, :], axis=1)
    flat = panels.transpose(1, 0, 2).reshape(half, own * width)
    partial = jnp.dot(all_rows, flat, preferred_element_type=jnp.float32)
    logits = lax.psum(partial, "sub")
    grad = jnp.where(present, jax.nn.sigmoid(logits) - target.astype(jnp.float32), 0.0)
    grad = grad.astype(jnp.bfloat16)
    back = lax.dot_general(
        grad, flat, (((1,), (1,)), ((), ())), preferred_element_type=jnp.float32
    ).astype(jnp.bfloat16)
    returned = lax.all_to_all(
        back.reshape(labs, samples, half), "lab", split_axis=0, concat_axis=0, tiled=True
    )
    enc_grad = jnp.sum(returned, axis=0, dtype=jnp.float32).astype(jnp.bfloat16)
    part = jnp.einsum(
        "rh,rcb->chb",
        all_rows,
        grad.reshape(labs * samples, own, width),
        preferred_element_type=jnp.float32,
    )
    panel_grad = lax.psum_scatter(part, "dp", scatter_dimension=0, tiled=True)
    return enc_grad, panel_grad


CUTS = 2
MESH = pl.DeviceIdType.MESH


def unit_of(u, me, labs):
    lefts, rights = me, labs - 1 - me
    p = u - CUTS
    both = 2 * jnp.minimum(lefts, rights)
    paired = p < 2 * both
    side = jnp.where(paired, p % 2, jnp.where(rights > lefts, 1, 0))
    s = jnp.where(paired, p // 2, p - both)
    count = jnp.where(side == 1, rights, lefts)
    near = s < count
    far_off = jnp.where(near, s + 1, 2 * count - s)
    block = jnp.where(u < CUTS, me, me + (2 * side - 1) * far_off)
    cut = jnp.where(u < CUTS, u, jnp.where(near, 0, 1))
    return block, cut


def step_kernel(
    dims, enc_ref, ids_ref, panel_ref, enc_out, panel_out,
    rows, rows_t, ids_buf, part, other, want, grads, held, sent, got, share_out, share_in,
    row_send, row_recv, id_send, id_recv, lx_send, lx_recv, rt_send, rt_recv, sh_send, sh_recv,
):
    labs, dps, own, beam, picks, width = dims
    size = enc_ref.shape[1]
    half = enc_ref.shape[2]
    me = lax.axis_index("lab")
    dp = lax.axis_index("dp")
    core = lax.axis_index("sub")
    left, right = jnp.maximum(me - 1, 0), jnp.minimum(me + 1, labs - 1)
    keep = own // dps
    last_right, cut_right = left, jnp.where(me == 0, 0, 1)
    last_left, cut_left = right, jnp.where(me == labs - 1, 0, 1)

    barrier = pltpu.get_barrier_semaphore()
    for off in range(1, labs):
        pl.semaphore_signal(barrier, inc=1, device_id={"lab": (me + off) % labs}, device_id_type=MESH)
    for off in range(1, dps):
        pl.semaphore_signal(barrier, inc=1, device_id={"dp": (dp + off) % dps}, device_id_type=MESH)
    pl.semaphore_signal(barrier, inc=1, device_id={"sub": 1 - core}, device_id_type=MESH)
    pl.semaphore_wait(barrier, labs + dps - 1)

    def remote(src, dst, send, recv, where):
        return pltpu.make_async_remote_copy(
            src_ref=src, dst_ref=dst, send_sem=send, recv_sem=recv,
            device_id=where, device_id_type=MESH,
        )

    def row_copy(src, block, cut, side):
        return remote(
            src, rows.at[block, cut], row_send.at[side, block, cut], row_recv.at[block, cut],
            {"lab": left if side == 0 else right},
        )

    def id_copy(off):
        return remote(
            ids_ref, ids_buf.at[me], id_send.at[off], id_recv.at[me], {"lab": (me + off) % labs}
        )

    def id_arrival(block):
        return remote(ids_ref, ids_buf.at[block], id_send.at[0], id_recv.at[block], {"lab": left})

    def lx_copy(block, cut):
        return remote(
            part.at[block, cut], other.at[block, cut],
            lx_send.at[block, cut], lx_recv.at[block, cut], {"sub": 1 - core},
        )

    def back_copy(block, cut, side):
        return remote(
            sent.at[block, cut], got.at[side, block, cut],
            rt_send.at[block, cut], rt_recv.at[side, block, cut],
            {"lab": right if side == 0 else left},
        )

    def share_copy(off, j):
        return remote(
            share_out.at[off - 1, j], share_in.at[off - 1, j],
            sh_send.at[off - 1, j], sh_recv.at[off - 1, j], {"dp": (dp + off) % dps},
        )

    for off in range(1, labs):
        id_copy(off).start()
    @pl.when(me > 0)
    def _():
        row_copy(enc_ref.at[0], me, 0, 0).start()

    @pl.when(me < labs - 1)
    def _():
        row_copy(enc_ref.at[0], me, 0, 1).start()

    rows[me] = enc_ref[...]
    ids_buf[me] = ids_ref[...]
    lane = lax.broadcasted_iota(jnp.int32, (1, width), 1).astype(jnp.float32)

    @pl.loop(0, labs * CUTS)
    def _(u):
        block, cut = unit_of(u, me, labs)

        @pl.when(block != me)
        def _():
            row_copy(enc_ref.at[0], block, cut, 0).wait_recv()

        @pl.when((block < me) & (me < labs - 1))
        def _():
            row_copy(rows.at[block, cut], block, cut, 1).start()

        @pl.when((block > me) & (me > 0))
        def _():
            row_copy(rows.at[block, cut], block, cut, 0).start()

        unit = rows[block, cut]
        for c in range(own):
            part[block, cut, :, c * width:(c + 1) * width] = jnp.dot(
                unit, panel_ref[c], preferred_element_type=jnp.float32
            )
        lx_copy(block, cut).start()
        rows_t[block, cut] = unit.T

        @pl.when((block != me) & (cut == 0))
        def _():
            id_arrival(block).wait_recv()

        ids = ids_buf[block, cut]
        ids = jnp.concatenate([ids, jnp.zeros((128 - ids.shape[0], size), jnp.float32)], axis=0).T
        for c in range(own):
            slot = (me * own + c).astype(jnp.float32)
            present = jnp.zeros((size, 1), jnp.bool_)
            for k in range(beam):
                present = present | (ids[:, k:k + 1] == slot)
            here = lane + slot * width
            target = jnp.zeros((size, width), jnp.float32)
            for i in range(beam, beam + picks):
                target = jnp.where(ids[:, i:i + 1] == here, 1.0, target)
            want[:, c * width:(c + 1) * width] = jnp.where(present, target, 2.0)

        lx_copy(block, cut).wait_recv()
        total = jnp.zeros((size, half), jnp.float32)
        for c in range(own):
            cols = slice(c * width, (c + 1) * width)
            logit = part[block, cut, :, cols] + other[block, cut, :, cols]
            goal = want[:, cols]
            grad = jnp.where(goal > 1.5, 0.0, jax.nn.sigmoid(logit) - goal).astype(jnp.bfloat16)
            grads[block, cut, :, cols] = grad
            total += lax.dot_general(
                grad, panel_ref[c], (((1,), (1,)), ((), ())), preferred_element_type=jnp.float32
            )
        held[block, cut] = total

        @pl.when((me == 0) & (block > 0))
        def _():
            sent[block, cut] = total.astype(jnp.bfloat16)
            back_copy(block, cut, 0).start()

        @pl.when((me == labs - 1) & (block < me))
        def _():
            sent[block, cut] = total.astype(jnp.bfloat16)
            back_copy(block, cut, 1).start()

        @pl.when((me < labs - 1) & (block == last_right) & (cut == cut_right))
        def _():
            row_copy(enc_ref.at[0], block, cut, 1).wait_send()
            row_copy(enc_ref.at[1], me, 1, 1).start()

        @pl.when((me > 0) & (block == last_left) & (cut == cut_left))
        def _():
            row_copy(enc_ref.at[0], block, cut, 0).wait_send()
            row_copy(enc_ref.at[1], me, 1, 0).start()

    units = [(b, q) for b in range(labs) for q in range(CUTS)]

    def panel_sum(c):
        wide = jnp.concatenate([rows_t[b, q] for b, q in units], axis=1)
        tall = jnp.concatenate(
            [grads[b, q, :, pl.ds(pl.multiple_of(c * width, width), width)] for b, q in units],
            axis=0,
        )
        return jnp.dot(wide, tall, preferred_element_type=jnp.float32)

    def pass_on(block, cut, side):
        back_copy(block, cut, side).wait_recv()
        sent[block, cut] = (
            held[block, cut] + got[side, block, cut].astype(jnp.float32)
        ).astype(jnp.bfloat16)
        back_copy(block, cut, side).start()

    def pass_all(k, cut):
        @pl.when((me > 0) & (me < k))
        def _():
            pass_on(k, cut, 0)

        @pl.when((me > labs - 1 - k) & (me < labs - 1))
        def _():
            pass_on(labs - 1 - k, cut, 1)

    for k in range(1, labs):
        pass_all(k, 0)
    for off in range(1, dps):
        for j in range(keep):
            share_out[off - 1, j] = panel_sum(((dp + off) % dps) * keep + j).astype(jnp.bfloat16)
            share_copy(off, j).start()
    for k in range(labs - 1, 0, -1):
        pass_all(k, 1)
    for j in range(keep):
        panel_out[j] = panel_sum(dp * keep + j)

    for cut in range(CUTS):
        @pl.when(me > 0)
        def _():
            back_copy(me, cut, 0).wait_recv()
            held[me, cut] += got[0, me, cut].astype(jnp.float32)

        @pl.when(me < labs - 1)
        def _():
            back_copy(me, cut, 1).wait_recv()
            held[me, cut] += got[1, me, cut].astype(jnp.float32)

        enc_out[cut] = held[me, cut].astype(jnp.bfloat16)

    for off in range(1, dps):
        for j in range(keep):
            share_copy(off, j).wait_recv()
            panel_out[j] += share_in[off - 1, j].astype(jnp.float32)

    for off in range(1, labs):
        id_copy(off).wait_send()
    for off in range(1, dps):
        for j in range(keep):
            share_copy(off, j).wait_send()
    for block, cut in units:
        lx_copy(block, cut).wait_send()

        @pl.when((block <= me) & (me < labs - 1) & ((block != last_right) | (cut != cut_right)))
        def _():
            row_copy(enc_ref.at[0], block, cut, 1).wait_send()

        @pl.when((block >= me) & (me > 0) & ((block != last_left) | (cut != cut_left)))
        def _():
            row_copy(enc_ref.at[0], block, cut, 0).wait_send()

        @pl.when(block != me)
        def _():
            back_copy(block, cut, 0).wait_send()


def kernel_body(enc_rows, shortlist, cluster_slot, positives, panels):
    samples, half = enc_rows.shape
    own, _, width = panels.shape
    labs, dps = lax.axis_size("lab"), lax.axis_size("dp")
    beam, picks = shortlist.shape[1], positives.shape[1]
    size = samples // CUTS
    keep = own // dps
    slots, pos_slot, pos_col = label_slots(shortlist, cluster_slot, positives, width)
    ids = jnp.concatenate([slots, pos_slot * width + pos_col], axis=1).astype(jnp.float32)
    id_rows = -(-(beam + picks) // 8) * 8
    ids = jnp.pad(ids, ((0, 0), (0, id_rows - beam - picks)), constant_values=-1.0)
    ids = ids.reshape(CUTS, size, id_rows).transpose(0, 2, 1)
    f32, bf16 = jnp.float32, jnp.bfloat16
    vmem, dma = pltpu.VMEM, pltpu.SemaphoreType.DMA
    whole = pl.BlockSpec(memory_space=pltpu.VMEM)
    enc_grad, panel_grad = pl.pallas_call(
        functools.partial(step_kernel, (labs, dps, own, beam, picks, width)),
        out_shape=(
            jax.ShapeDtypeStruct((CUTS, size, half), bf16),
            jax.ShapeDtypeStruct((keep, half, width), f32),
        ),
        in_specs=[whole] * 3,
        out_specs=(whole, whole),
        scratch_shapes=[
            vmem((labs, CUTS, size, half), bf16),
            vmem((labs, CUTS, half, size), bf16),
            vmem((labs, CUTS, id_rows, size), f32),
            vmem((labs, CUTS, size, own * width), f32),
            vmem((labs, CUTS, size, own * width), f32),
            vmem((size, own * width), f32),
            vmem((labs, CUTS, size, own * width), bf16),
            vmem((labs, CUTS, size, half), f32),
            vmem((labs, CUTS, size, half), bf16),
            vmem((2, labs, CUTS, size, half), bf16),
            vmem((dps - 1, keep, half, width), bf16),
            vmem((dps - 1, keep, half, width), bf16),
            dma((2, labs, CUTS)),
            dma((labs, CUTS)),
            dma((labs,)),
            dma((labs,)),
            dma((labs, CUTS)),
            dma((labs, CUTS)),
            dma((labs, CUTS)),
            dma((2, labs, CUTS)),
            dma((dps - 1, keep)),
            dma((dps - 1, keep)),
        ],
        compiler_params=pltpu.CompilerParams(
            collective_id=0, has_side_effects=True, vmem_limit_bytes=58 << 20
        ),
    )(enc_rows.reshape(CUTS, size, half), ids, panels)
    return enc_grad.reshape(samples, half), panel_grad


def kernel_fits(enc_rows, shortlist, positives, panels):
    samples, half = enc_rows.shape
    own, _, width = panels.shape
    labs, dps = lax.axis_size("lab"), lax.axis_size("dp")
    unit = labs * samples
    room = unit * half * 14 + unit * own * width * 10 + 14 * own * half * width
    return (
        room < 54 << 20
        and labs > 1
        and dps > 1
        and lax.axis_size("sub") == 2
        and own % dps == 0
        and samples % (CUTS * 128) == 0
        and half % 128 == 0
        and width % 128 == 0
        and shortlist.shape[1] + positives.shape[1] <= 128
    )


def body(enc_rows, shortlist, cluster_slot, positives, panels):
    if kernel_fits(enc_rows, shortlist, positives, panels):
        return kernel_body(enc_rows, shortlist, cluster_slot, positives, panels)
    return array_body(enc_rows, shortlist, cluster_slot, positives, panels)


def solution(mesh):
    in_specs = (
        P(("grp", "lab", "dp"), "sub"),
        P(("grp", "lab", "dp"), None),
        P(),
        P(("grp", "lab", "dp"), None),
        P("lab", "sub", None),
    )
    out_specs = (P(("grp", "lab", "dp"), "sub"), P(("grp", "lab", "dp"), "sub", None))
    return jax.shard_map(body, mesh=mesh, in_specs=in_specs, out_specs=out_specs, check_vma=False)
```

```python
import functools

import jax
import jax.numpy as jnp
from jax import lax
from jax.experimental import pallas as pl
from jax.experimental.pallas import tpu as pltpu
from jax.sharding import PartitionSpec as P


def label_slots(shortlist, cluster_slot, positives, label_width):
    clusters = jnp.arange(cluster_slot.shape[0], dtype=jnp.int32)
    named = (shortlist[:, :, None] == clusters).astype(jnp.int32)
    slots = jnp.sum(named * cluster_slot, axis=2)
    beams = jnp.arange(shortlist.shape[1], dtype=jnp.int32)
    picked = (positives[:, :, None] // label_width == beams).astype(jnp.int32)
    pos_slot = jnp.sum(picked * slots[:, None, :], axis=2)
    return slots, pos_slot, positives % label_width


def array_body(enc_rows, shortlist, cluster_slot, positives, panels):
    samples, half = enc_rows.shape
    own, _, width = panels.shape
    labs = lax.axis_size("lab")
    slots, pos_slot, pos_col = label_slots(shortlist, cluster_slot, positives, width)
    ids = jnp.concatenate([slots, pos_slot * width + pos_col], axis=1)
    all_ids = lax.all_gather(ids, "lab", axis=0, tiled=True)
    all_rows = lax.all_gather(enc_rows, "lab", axis=0, tiled=True)
    beam = shortlist.shape[1]
    first = lax.axis_index("lab") * own
    columns = first * width + jnp.arange(own * width, dtype=jnp.int32)
    present = jnp.any(all_ids[:, :beam, None] == columns[None, None, :] // width, axis=1)
    target = jnp.any(all_ids[:, beam:, None] == columns[None, None, :], axis=1)
    flat = panels.transpose(1, 0, 2).reshape(half, own * width)
    partial = jnp.dot(all_rows, flat, preferred_element_type=jnp.float32)
    logits = lax.psum(partial, "sub")
    grad = jnp.where(present, jax.nn.sigmoid(logits) - target.astype(jnp.float32), 0.0)
    grad = grad.astype(jnp.bfloat16)
    back = lax.dot_general(
        grad, flat, (((1,), (1,)), ((), ())), preferred_element_type=jnp.float32
    ).astype(jnp.bfloat16)
    returned = lax.all_to_all(
        back.reshape(labs, samples, half), "lab", split_axis=0, concat_axis=0, tiled=True
    )
    enc_grad = jnp.sum(returned, axis=0, dtype=jnp.float32).astype(jnp.bfloat16)
    part = jnp.einsum(
        "rh,rcb->chb",
        all_rows,
        grad.reshape(labs * samples, own, width),
        preferred_element_type=jnp.float32,
    )
    panel_grad = lax.psum_scatter(part, "dp", scatter_dimension=0, tiled=True)
    return enc_grad, panel_grad


CUTS = 2
MESH = pl.DeviceIdType.MESH


def unit_of(u, me, labs):
    lefts, rights = me, labs - 1 - me
    p = u - CUTS
    both = 2 * jnp.minimum(lefts, rights)
    paired = p < 2 * both
    side = jnp.where(paired, p % 2, jnp.where(rights > lefts, 1, 0))
    s = jnp.where(paired, p // 2, p - both)
    count = jnp.where(side == 1, rights, lefts)
    near = s < count
    far_off = jnp.where(near, s + 1, 2 * count - s)
    block = jnp.where(u < CUTS, me, me + (2 * side - 1) * far_off)
    cut = jnp.where(u < CUTS, u, jnp.where(near, 0, 1))
    return block, cut


def step_kernel(
    dims, enc_ref, ids_ref, panel_ref, enc_out, panel_out,
    rows, rows_t, ids_buf, part, other, want, grads, held, sent, got, share_out, share_in,
    row_send, row_recv, id_send, id_recv, lx_send, lx_recv, rt_send, rt_recv, sh_send, sh_recv,
):
    labs, dps, own, beam, picks, width = dims
    size = enc_ref.shape[1]
    half = enc_ref.shape[2]
    me = lax.axis_index("lab")
    dp = lax.axis_index("dp")
    core = lax.axis_index("sub")
    left, right = jnp.maximum(me - 1, 0), jnp.minimum(me + 1, labs - 1)
    keep = own // dps
    last_right, cut_right = left, jnp.where(me == 0, 0, 1)
    last_left, cut_left = right, jnp.where(me == labs - 1, 0, 1)
    lefts, rights = me, labs - 1 - me
    near_left = lefts <= rights
    right_turn = jnp.where(me == 0, 0, jnp.where(near_left, CUTS + 4 * lefts - 1, -1))
    left_turn = jnp.where(rights == 0, 0, jnp.where(near_left, -1, CUTS + 4 * rights))

    barrier = pltpu.get_barrier_semaphore()
    for off in range(1, labs):
        pl.semaphore_signal(barrier, inc=1, device_id={"lab": (me + off) % labs}, device_id_type=MESH)
    for off in range(1, dps):
        pl.semaphore_signal(barrier, inc=1, device_id={"dp": (dp + off) % dps}, device_id_type=MESH)
    pl.semaphore_signal(barrier, inc=1, device_id={"sub": 1 - core}, device_id_type=MESH)
    pl.semaphore_wait(barrier, labs + dps - 1)

    def remote(src, dst, send, recv, where):
        return pltpu.make_async_remote_copy(
            src_ref=src, dst_ref=dst, send_sem=send, recv_sem=recv,
            device_id=where, device_id_type=MESH,
        )

    def row_copy(src, block, cut, side):
        return remote(
            src, rows.at[block, cut], row_send.at[side, block, cut], row_recv.at[block, cut],
            {"lab": left if side == 0 else right},
        )

    def id_copy(off):
        return remote(
            ids_ref, ids_buf.at[me], id_send.at[off], id_recv.at[me], {"lab": (me + off) % labs}
        )

    def id_arrival(block):
        return remote(ids_ref, ids_buf.at[block], id_send.at[0], id_recv.at[block], {"lab": left})

    def lx_copy(block, cut):
        return remote(
            part.at[block, cut], other.at[block, cut],
            lx_send.at[block, cut], lx_recv.at[block, cut], {"sub": 1 - core},
        )

    def back_copy(block, cut, side):
        return remote(
            sent.at[block, cut], got.at[side, block, cut],
            rt_send.at[block, cut], rt_recv.at[side, block, cut],
            {"lab": right if side == 0 else left},
        )

    def share_copy(off, j):
        return remote(
            share_out.at[off - 1, j], share_in.at[off - 1, j],
            sh_send.at[off - 1, j], sh_recv.at[off - 1, j], {"dp": (dp + off) % dps},
        )

    def late_half(side):
        block, cut = (last_left, cut_left) if side == 0 else (last_right, cut_right)
        row_copy(enc_ref.at[0], block, cut, side).wait_send()
        row_copy(enc_ref.at[1], me, 1, side).start()

    for off in range(1, labs):
        id_copy(off).start()
    @pl.when(me > 0)
    def _():
        row_copy(enc_ref.at[0], me, 0, 0).start()

    @pl.when(me < labs - 1)
    def _():
        row_copy(enc_ref.at[0], me, 0, 1).start()

    rows[me] = enc_ref[...]
    ids_buf[me] = ids_ref[...]
    lane = lax.broadcasted_iota(jnp.int32, (1, width), 1).astype(jnp.float32)

    @pl.loop(0, labs * CUTS)
    def _(u):
        block, cut = unit_of(u, me, labs)

        @pl.when(block != me)
        def _():
            row_copy(enc_ref.at[0], block, cut, 0).wait_recv()

        @pl.when((block < me) & (me < labs - 1))
        def _():
            row_copy(rows.at[block, cut], block, cut, 1).start()

        @pl.when((block > me) & (me > 0))
        def _():
            row_copy(rows.at[block, cut], block, cut, 0).start()

        unit = rows[block, cut]
        for c in range(own):
            part[block, cut, :, c * width:(c + 1) * width] = jnp.dot(
                unit, panel_ref[c], preferred_element_type=jnp.float32
            )
        lx_copy(block, cut).start()
        rows_t[block, cut] = unit.T

        @pl.when((block != me) & (cut == 0))
        def _():
            id_arrival(block).wait_recv()

        ids = ids_buf[block, cut]
        ids = jnp.concatenate([ids, jnp.zeros((128 - ids.shape[0], size), jnp.float32)], axis=0).T
        for c in range(own):
            slot = (me * own + c).astype(jnp.float32)
            present = jnp.zeros((size, 1), jnp.bool_)
            for k in range(beam):
                present = present | (ids[:, k:k + 1] == slot)
            here = lane + slot * width
            target = jnp.zeros((size, width), jnp.float32)
            for i in range(beam, beam + picks):
                target = jnp.where(ids[:, i:i + 1] == here, 1.0, target)
            want[:, c * width:(c + 1) * width] = jnp.where(present, target, 2.0)

        lx_copy(block, cut).wait_recv()
        total = jnp.zeros((size, half), jnp.float32)
        for c in range(own):
            cols = slice(c * width, (c + 1) * width)
            logit = part[block, cut, :, cols] + other[block, cut, :, cols]
            goal = want[:, cols]
            grad = jnp.where(goal > 1.5, 0.0, jax.nn.sigmoid(logit) - goal).astype(jnp.bfloat16)
            grads[block, cut, :, cols] = grad
            total += lax.dot_general(
                grad, panel_ref[c], (((1,), (1,)), ((), ())), preferred_element_type=jnp.float32
            )
        held[block, cut] = total

        @pl.when((me == 0) & (block > 0))
        def _():
            sent[block, cut] = total.astype(jnp.bfloat16)
            back_copy(block, cut, 0).start()

        @pl.when((me == labs - 1) & (block < me))
        def _():
            sent[block, cut] = total.astype(jnp.bfloat16)
            back_copy(block, cut, 1).start()

        @pl.when((me < labs - 1) & (u == right_turn))
        def _():
            late_half(1)

        @pl.when((me > 0) & (u == left_turn))
        def _():
            late_half(0)

    units = [(b, q) for b in range(labs) for q in range(CUTS)]

    def panel_sum(c):
        wide = jnp.concatenate([rows_t[b, q] for b, q in units], axis=1)
        tall = jnp.concatenate(
            [grads[b, q, :, pl.ds(pl.multiple_of(c * width, width), width)] for b, q in units],
            axis=0,
        )
        return jnp.dot(wide, tall, preferred_element_type=jnp.float32)

    def pass_on(block, cut, side):
        back_copy(block, cut, side).wait_recv()
        sent[block, cut] = (
            held[block, cut] + got[side, block, cut].astype(jnp.float32)
        ).astype(jnp.bfloat16)
        back_copy(block, cut, side).start()

    def pass_right(k, cut):
        @pl.when((me > 0) & (me < k))
        def _():
            pass_on(k, cut, 0)

    def pass_left(k, cut):
        @pl.when((me > labs - 1 - k) & (me < labs - 1))
        def _():
            pass_on(labs - 1 - k, cut, 1)

    @pl.when(near_left)
    def _():
        for k in range(1, labs):
            pass_right(k, 0)

        @pl.when(me > 0)
        def _():
            late_half(0)

        for k in range(1, labs):
            pass_left(k, 0)

    @pl.when(jnp.logical_not(near_left))
    def _():
        for k in range(1, labs):
            pass_left(k, 0)

        @pl.when(me < labs - 1)
        def _():
            late_half(1)

        for k in range(1, labs):
            pass_right(k, 0)

    for off in range(1, dps):
        for j in range(keep):
            share_out[off - 1, j] = panel_sum(((dp + off) % dps) * keep + j).astype(jnp.bfloat16)
            share_copy(off, j).start()
    for k in range(labs - 1, 0, -1):
        pass_right(k, 1)
        pass_left(k, 1)
    for j in range(keep):
        panel_out[j] = panel_sum(dp * keep + j)

    for cut in range(CUTS):
        @pl.when(me > 0)
        def _():
            back_copy(me, cut, 0).wait_recv()
            held[me, cut] += got[0, me, cut].astype(jnp.float32)

        @pl.when(me < labs - 1)
        def _():
            back_copy(me, cut, 1).wait_recv()
            held[me, cut] += got[1, me, cut].astype(jnp.float32)

        enc_out[cut] = held[me, cut].astype(jnp.bfloat16)

    for off in range(1, dps):
        for j in range(keep):
            share_copy(off, j).wait_recv()
            panel_out[j] += share_in[off - 1, j].astype(jnp.float32)

    for off in range(1, labs):
        id_copy(off).wait_send()
    for off in range(1, dps):
        for j in range(keep):
            share_copy(off, j).wait_send()
    for block, cut in units:
        lx_copy(block, cut).wait_send()

        @pl.when((block <= me) & (me < labs - 1) & ((block != last_right) | (cut != cut_right)))
        def _():
            row_copy(enc_ref.at[0], block, cut, 1).wait_send()

        @pl.when((block >= me) & (me > 0) & ((block != last_left) | (cut != cut_left)))
        def _():
            row_copy(enc_ref.at[0], block, cut, 0).wait_send()

        @pl.when(block != me)
        def _():
            back_copy(block, cut, 0).wait_send()


def kernel_body(enc_rows, shortlist, cluster_slot, positives, panels):
    samples, half = enc_rows.shape
    own, _, width = panels.shape
    labs, dps = lax.axis_size("lab"), lax.axis_size("dp")
    beam, picks = shortlist.shape[1], positives.shape[1]
    size = samples // CUTS
    keep = own // dps
    slots, pos_slot, pos_col = label_slots(shortlist, cluster_slot, positives, width)
    ids = jnp.concatenate([slots, pos_slot * width + pos_col], axis=1).astype(jnp.float32)
    id_rows = -(-(beam + picks) // 8) * 8
    ids = jnp.pad(ids, ((0, 0), (0, id_rows - beam - picks)), constant_values=-1.0)
    ids = ids.reshape(CUTS, size, id_rows).transpose(0, 2, 1)
    f32, bf16 = jnp.float32, jnp.bfloat16
    vmem, dma = pltpu.VMEM, pltpu.SemaphoreType.DMA
    whole = pl.BlockSpec(memory_space=pltpu.VMEM)
    enc_grad, panel_grad = pl.pallas_call(
        functools.partial(step_kernel, (labs, dps, own, beam, picks, width)),
        out_shape=(
            jax.ShapeDtypeStruct((CUTS, size, half), bf16),
            jax.ShapeDtypeStruct((keep, half, width), f32),
        ),
        in_specs=[whole] * 3,
        out_specs=(whole, whole),
        scratch_shapes=[
            vmem((labs, CUTS, size, half), bf16),
            vmem((labs, CUTS, half, size), bf16),
            vmem((labs, CUTS, id_rows, size), f32),
            vmem((labs, CUTS, size, own * width), f32),
            vmem((labs, CUTS, size, own * width), f32),
            vmem((size, own * width), f32),
            vmem((labs, CUTS, size, own * width), bf16),
            vmem((labs, CUTS, size, half), f32),
            vmem((labs, CUTS, size, half), bf16),
            vmem((2, labs, CUTS, size, half), bf16),
            vmem((dps - 1, keep, half, width), bf16),
            vmem((dps - 1, keep, half, width), bf16),
            dma((2, labs, CUTS)),
            dma((labs, CUTS)),
            dma((labs,)),
            dma((labs,)),
            dma((labs, CUTS)),
            dma((labs, CUTS)),
            dma((labs, CUTS)),
            dma((2, labs, CUTS)),
            dma((dps - 1, keep)),
            dma((dps - 1, keep)),
        ],
        compiler_params=pltpu.CompilerParams(
            collective_id=0, has_side_effects=True, vmem_limit_bytes=58 << 20
        ),
    )(enc_rows.reshape(CUTS, size, half), ids, panels)
    return enc_grad.reshape(samples, half), panel_grad


def kernel_fits(enc_rows, shortlist, positives, panels):
    samples, half = enc_rows.shape
    own, _, width = panels.shape
    labs, dps = lax.axis_size("lab"), lax.axis_size("dp")
    unit = labs * samples
    room = unit * half * 14 + unit * own * width * 10 + 14 * own * half * width
    return (
        room < 54 << 20
        and labs > 1
        and dps > 1
        and lax.axis_size("sub") == 2
        and own % dps == 0
        and samples % (CUTS * 128) == 0
        and half % 128 == 0
        and width % 128 == 0
        and shortlist.shape[1] + positives.shape[1] <= 128
    )


def body(enc_rows, shortlist, cluster_slot, positives, panels):
    if kernel_fits(enc_rows, shortlist, positives, panels):
        return kernel_body(enc_rows, shortlist, cluster_slot, positives, panels)
    return array_body(enc_rows, shortlist, cluster_slot, positives, panels)


def solution(mesh):
    in_specs = (
        P(("grp", "lab", "dp"), "sub"),
        P(("grp", "lab", "dp"), None),
        P(),
        P(("grp", "lab", "dp"), None),
        P("lab", "sub", None),
    )
    out_specs = (P(("grp", "lab", "dp"), "sub"), P(("grp", "lab", "dp"), "sub", None))
    return jax.shard_map(body, mesh=mesh, in_specs=in_specs, out_specs=out_specs, check_vma=False)
```
